512 devices in a mesh: light: 16 (over y, x), view: 32 (over z, core).
Axes of the slice: x: 4, y: 4, z: 16, core: 2. Of those that a mesh axis runs over, the one named last changes fastest.
Arguments:
- density: float32 [128, 256, 2048], P('light', 'view'), may hold values from 0.1 to 2
- albedo: bfloat16 [3, 128, 256, 2048], P(None, 'light', 'view'), may hold values from 0.099609375 to 1
- light_color: float32 [8, 3], replicated, may hold values from 0.5 to 1.5
- light_shift: int32 [8], replicated, may hold values from -1 to 1
- view_flip: int32 [128], P('light'), may hold values 0 or 1
Outputs:
- images: float32 [8, 4, 262144], P(None, None, ('light', 'view'))
The draws below stay inside these ranges and needn't reach their ends.
Inputs may be any that keep to these rules, and one draw needn't show every extreme that they name: `light_shift`: every light steps sideways by at most one cell per slice. `view_flip`: 0 means lower view indices lie in front, 1 means higher ones do.
All inputs are finite; a program needn't handle non-finite values. No bound on the sum of `view_flip` on one device may be relied on, other than what follows from the above.
Results may differ from the reference program's by a relative error of at most 0.0003.
Values sent between devices are 32-bit elements; how exact they have to be, the bound alone decides.
No kernel may reach another device: no remote copies, remote signals or barrier semaphores. Data moves between devices by JAX's collectives and lax.ppermute only.
A program may use at most 64 MiB of HBM per device.

```python
import math
import jax
import jax.numpy as jnp
from jax import lax

W = 2048
LIGHTS = 8
NX = 128
NY = 256


def set_ends(result, key, low, top_value):
    longest = result.shape.index(max(result.shape))
    spots = []
    for shift in (0, 1):
        where = [jax.random.randint(jax.random.fold_in(key, axis), (), 0, length) for axis, length in enumerate(result.shape)]
        where[longest] = (where[longest] + shift) % result.shape[longest]
        spots.append(tuple(where))
    return result.at[spots[0]].set(low).at[spots[1]].set(top_value)


def steps_of(own_key, extent, shards, low, largest):
    def one(position, parts):
        steps = jax.random.uniform(jax.random.fold_in(jax.random.fold_in(own_key, 6), position), (parts,), jnp.float32, low / len(shards), largest / len(shards))
        return jnp.repeat(jnp.exp(steps), extent[position] // parts).reshape((-1,) + (1,) * (len(extent) - position - 1))

    gain = one(*shards[0])
    for cut in shards[1:]:
        gain = gain * one(*cut)
    return gain


def setup_inputs(seed: int = 0) -> dict:
    keys = jax.random.split(jax.random.key(seed), 6)
    density = jnp.clip(jnp.exp(math.log(2.0) - 2.9957323 * jax.random.uniform(keys[0], (NX, NY, W), jnp.float32) ** steps_of(keys[0], (NX, NY, W), ((0, 16), (1, 32)), -0.2, 0.2)), 0.1, 2.0)
    albedo = jnp.clip(0.099609375 + 0.9003906 * jax.random.uniform(keys[1], (3, NX, NY, W), jnp.float32) ** steps_of(keys[1], (3, NX, NY, W), ((1, 16), (2, 32)), -0.2, 0.2), 0.099609375, 1.0).astype(jnp.bfloat16)
    light_color = jnp.clip(jax.random.uniform(keys[2], (LIGHTS, 3), jnp.float32, 0.5, 1.5), 0.5, 1.5)
    light_shift = set_ends(jax.random.randint(keys[3], (LIGHTS,), -1, 2), jax.random.fold_in(keys[3], 1), -1, 1).astype(jnp.int32)
    view_flip = set_ends((jax.random.randint(keys[4], (NX,), 0, 2) < 1).astype(jnp.int32), jax.random.fold_in(keys[4], 1), 0, 1)
    return {"density": density, "albedo": albedo, "light_color": light_color, "light_shift": light_shift, "view_flip": view_flip}


LIGHT_DEPTH = 1.5
VIEW_DEPTH = 2.0


def shift_cells(planes, lateral):
    columns = planes.shape[-1]
    source = jnp.arange(columns, dtype=jnp.int32) - lateral
    inside = (source >= 0) & (source < columns)
    clipped = jnp.broadcast_to(jnp.clip(source, 0, columns - 1), planes.shape)
    picked = jnp.take_along_axis(planes, clipped, axis=-1)
    return jnp.where(inside, picked, jnp.ones_like(picked))


def reference(density, albedo, light_color, light_shift, view_flip):
    rows_total, cells, columns = density.shape
    light_step = LIGHT_DEPTH / rows_total
    view_step = VIEW_DEPTH / cells
    images = []
    for light_id in range(LIGHTS):
        lateral = light_shift[light_id]
        light_tint = light_color[light_id].astype(jnp.float32)

        def march_step(transmit, row_index):
            density_row = density[row_index]
            reflect = albedo[:, row_index].astype(jnp.float32)
            depth_view = density_row * view_step
            running = jnp.cumsum(depth_view, axis=0)
            column_total = running[-1]
            ahead_depth = jnp.where(view_flip[row_index] == 1, column_total[None, :] - running, running - depth_view)
            weights = jnp.exp(-ahead_depth) * (1.0 - jnp.exp(-depth_view))
            colour = jnp.sum(reflect * (weights * transmit)[None], axis=1) * light_tint[:, None]
            opacity = 1.0 - jnp.exp(-column_total)
            image_row = jnp.concatenate([colour, opacity[None]], axis=0)
            return shift_cells(transmit * jnp.exp(-density_row * light_step), lateral), image_row

        _, image_rows = lax.scan(march_step, jnp.ones((cells, columns), jnp.float32), jnp.arange(rows_total, dtype=jnp.int32))
        images.append(jnp.transpose(image_rows, (1, 0, 2)).reshape(4, rows_total * columns))
    return jnp.stack(images)
```

```python
import jax
import jax.numpy as jnp
from jax import lax
from jax.experimental import pallas as pl
from jax.experimental.pallas import tpu as pltpu
from jax.sharding import PartitionSpec as P

LIGHTS = 8
LIGHT_DEPTH = 1.5
VIEW_DEPTH = 2.0
LANES = 128
STEPS = (-1, 0, 1)
ROWS = 40


def slide(planes, amount):
    if amount == 0:
        return planes
    columns = planes.shape[-1]
    rolled = pltpu.roll(planes, amount % columns, axis=1)
    lane = lax.broadcasted_iota(jnp.int32, (planes.shape[0], LANES), 1)
    if amount > 0:
        edge = jnp.where(lane >= amount, rolled[:, :LANES], 0.0)
        return jnp.concatenate([edge, rolled[:, LANES:]], axis=1)
    edge = jnp.where(lane < LANES + amount, rolled[:, columns - LANES :], 0.0)
    return jnp.concatenate([rolled[:, : columns - LANES], edge], axis=1)


def exit_kernel(scale, density_ref, exit_ref):
    slices, cells, columns = density_ref.shape
    for index, step in enumerate(STEPS):
        total = jnp.zeros((cells, columns), jnp.float32)
        for k in range(slices):
            total = slide(total + density_ref[k] * scale, step)
        exit_ref[index * cells : (index + 1) * cells, :] = total


def row_kernel(slices, rows_ref, total_ref):
    count, planes, columns = rows_ref.shape
    cells = planes // len(STEPS)
    for index, step in enumerate(STEPS):
        part = slice(index * cells, (index + 1) * cells)
        total = rows_ref[0, part, :]
        for x in range(1, count):
            total = slide(total, slices * step) + rows_ref[x, part, :]
        total_ref[part, :] = total


def gather_sums(parts, low):
    for bit, mask in enumerate(low):
        merged = []
        for i in range(0, len(parts), 2):
            a, b = parts[i], parts[i + 1]
            merged.append(jnp.where(mask, a, b) + pltpu.roll(jnp.where(mask, b, a), 1 << bit, axis=0))
        parts = merged
    return parts[0]


def brick_kernel(
    light_scale, view_scale, flip_ref, density_ref, albedo_ref, rows_ref, totals_ref, keep_ref, send_ref, depth_ref, lit_ref
):
    slices, cells, columns = density_ref.shape
    across = rows_ref.shape[0]
    light = lax.axis_index("light")
    place_x, place_y = lax.rem(light, across), light // across
    core = lax.rem(lax.axis_index("view"), 2)
    for index, step in enumerate(STEPS):
        part = slice(index * cells, (index + 1) * cells)
        entering = jnp.zeros((cells, columns), jnp.float32)
        for y in range(totals_ref.shape[0] - 1):
            entering = jnp.where(y < place_y, slide(entering, slices * across * step) + totals_ref[y, part, :], entering)
        for x in range(across - 1):
            entering = jnp.where(x < place_x, slide(entering, slices * step) + rows_ref[x, part, :], entering)
        depth_ref[index] = entering

    row = lax.broadcasted_iota(jnp.int32, (cells, LANES), 0)
    low = [(row & (1 << bit)) == 0 for bit in range(3)]
    row_wide = lax.broadcasted_iota(jnp.int32, (cells, columns), 0)
    mine_even = core == 0

    def one_slice(k, carry):
        dense = density_ref[k]
        flipped = flip_ref[k] == 1
        depth_view = dense * view_scale
        running = depth_view
        for reach in (1, 2, 4):
            running = running + jnp.where(row_wide >= reach, pltpu.roll(running, reach, axis=0), 0.0)
        total = jnp.broadcast_to(running[cells - 1 :, :], (cells, columns))
        ahead = jnp.where(flipped, total - running, running - depth_view)
        weights = jnp.exp(ahead) * (1.0 - jnp.exp(depth_view))
        dense_light = dense * light_scale
        for index, step in enumerate(STEPS):
            depth = depth_ref[index]
            lit_ref[index] = weights * jnp.exp(depth)
            depth_ref[index] = slide(depth + dense_light, step)
        for pair in range(columns // (8 * LANES)):
            chunks = []
            for chunk in (2 * pair, 2 * pair + 1):
                groups = [slice((4 * chunk + g) * LANES, (4 * chunk + g + 1) * LANES) for g in range(4)]
                reflect = [[albedo_ref[c, k, :, g].astype(jnp.float32) for g in groups] for c in range(3)]
                products = []
                for index in range(len(STEPS)):
                    lit = [lit_ref[index, :, g] for g in groups]
                    for c in range(3):
                        products += [reflect[c][g] * lit[g] for g in range(4)]
                products += [depth_view[:, g] for g in groups]
                tiles = [gather_sums(products[t : t + 8], low) for t in range(0, ROWS, 8)]
                tiles[-1] = jnp.where(low[2], tiles[-1], jnp.exp(jnp.where(low[2], 0.0, tiles[-1])))
                chunks.append(tiles)
            where = k * (columns // (8 * LANES)) + pair
            for t, (even, odd) in enumerate(zip(*chunks)):
                keep_ref[where, 8 * t : 8 * t + 8, :] = jnp.where(mine_even, even, odd)
                send_ref[where, 8 * t : 8 * t + 8, :] = jnp.where(mine_even, odd, even)
        return carry

    lax.fori_loop(0, slices, one_slice, 0)


def both_halves(tile, low):
    return jnp.where(low, pltpu.roll(tile, 4, axis=0), tile)


def over(front, back, low):
    through = both_halves(front[-1], low)
    out = [f + through * b for f, b in zip(front[:-1], back[:-1])]
    return out + [jnp.where(low, front[-1], 0.0) + through * back[-1]]


def tiles_of(ref, index):
    return [ref[index, 8 * t : 8 * t + 8, :] for t in range(ROWS // 8)]


def pair_kernel(per_slice, flip_ref, keep_ref, recv_ref, out_ref):
    low = lax.broadcasted_iota(jnp.int32, (8, LANES), 0) < 4
    core = lax.rem(lax.axis_index("view"), 2)

    def one_slice(k, carry):
        mine_front = core == flip_ref[k]
        for h in range(per_slice):
            where = k * per_slice + h
            keep, recv = tiles_of(keep_ref, where), tiles_of(recv_ref, where)
            front = [jnp.where(mine_front, a, b) for a, b in zip(keep, recv)]
            back = [jnp.where(mine_front, b, a) for a, b in zip(keep, recv)]
            for t, tile in enumerate(over(front, back, low)):
                out_ref[where, 8 * t : 8 * t + 8, :] = tile
        return carry

    lax.fori_loop(0, keep_ref.shape[0] // per_slice, one_slice, 0)


def final_kernel(per_slice, flip_ref, shift_ref, color_ref, pieces_ref, out_ref, sums_ref):
    low = lax.broadcasted_iota(jnp.int32, (8, LANES), 0) < 4
    count = pieces_ref.shape[0]
    flipped = flip_ref[lax.axis_index("view") // per_slice] == 1
    current = None
    for j in range(count):
        tiles = tiles_of(pieces_ref, jnp.where(flipped, count - 1 - j, j))
        current = tiles if current is None else over(current, tiles, low)
    for t, tile in enumerate(current):
        sums_ref[8 * t : 8 * t + 8, :] = tile
    for light in range(LIGHTS):
        base = (shift_ref[light] + 1) * 12
        for c in range(3):
            tint = color_ref[light, c]
            for g in range(4):
                out_ref[light, c : c + 1, g * LANES : (g + 1) * LANES] = sums_ref[pl.ds(base + 4 * c + g, 1), :] * tint
        for g in range(4):
            out_ref[light, 3:4, g * LANES : (g + 1) * LANES] = 1.0 - sums_ref[36 + g : 37 + g, :]


def vmem(count):
    return [pl.BlockSpec(memory_space=pltpu.VMEM)] * count


def smem(count):
    return [pl.BlockSpec(memory_space=pltpu.SMEM)] * count


def local(density, albedo, light_color, light_shift, view_flip):
    slices, cells, columns = density.shape
    light_count, view_count = lax.axis_size("light"), lax.axis_size("view")
    across = 4
    light_scale = -LIGHT_DEPTH / (slices * light_count)
    view_scale = -VIEW_DEPTH / (cells * view_count)
    planes = len(STEPS) * cells
    f32 = jnp.float32

    def call(kernel, name, out_shape, in_specs, scratch=()):
        many = isinstance(out_shape, (list, tuple))
        return pl.pallas_call(
            kernel,
            name=name,
            out_shape=out_shape,
            in_specs=in_specs,
            out_specs=vmem(len(out_shape)) if many else vmem(1)[0],
            scratch_shapes=scratch,
        )

    def shaped(*shape):
        return jax.ShapeDtypeStruct(shape, f32)

    rows_x = [[y * across + x for x in range(across)] for y in range(light_count // across)]
    rows_y = [[y * across + x for y in range(light_count // across)] for x in range(across)]
    leaving = call(lambda *refs: exit_kernel(light_scale, *refs), "exits", shaped(planes, columns), vmem(1))(density)
    in_row = lax.all_gather(leaving, "light", axis_index_groups=rows_x)
    total = call(lambda *refs: row_kernel(slices, *refs), "row_total", shaped(planes, columns), vmem(1))(in_row)
    totals = lax.all_gather(total, "light", axis_index_groups=rows_y)
    pieces = view_count // 2
    keep, send = call(
        lambda *refs: brick_kernel(light_scale, view_scale, *refs),
        "brick",
        [shaped(pieces, ROWS, LANES)] * 2,
        smem(1) + vmem(4),
        [pltpu.VMEM((len(STEPS), cells, columns), f32), pltpu.VMEM((len(STEPS), cells, columns), f32)],
    )(view_flip, density, albedo, in_row, totals)
    received = lax.ppermute(send, "view", [(v, v ^ 1) for v in range(view_count)])
    paired = call(
        lambda *refs: pair_kernel(pieces // slices, *refs), "pair", shaped(pieces, ROWS, LANES), smem(1) + vmem(2)
    )(view_flip, keep, received)
    groups = [[2 * z + c for z in range(pieces)] for c in range(2)]
    spread = lax.all_to_all(paired, "view", 0, 0, axis_index_groups=groups)
    return call(
        lambda *refs: final_kernel(view_count // slices, *refs),
        "final",
        shaped(LIGHTS, 4, slices * columns // view_count),
        smem(3) + vmem(1),
        [pltpu.VMEM((ROWS, LANES), f32)],
    )(view_flip, light_shift, light_color, spread)


def solution(mesh):
    return jax.shard_map(
        local,
        mesh=mesh,
        in_specs=(P("light", "view", None), P(None, "light", "view", None), P(), P(), P("light")),
        out_specs=P(None, None, ("light", "view")),
        check_vma=False,
    )
```

```python
import jax
import jax.numpy as jnp
from jax import lax
from jax.experimental import pallas as pl
from jax.experimental.pallas import tpu as pltpu
from jax.sharding import PartitionSpec as P

LIGHTS = 8
LIGHT_DEPTH = 1.5
VIEW_DEPTH = 2.0
LANES = 128
STEPS = (-1, 0, 1)
ROWS = 40


def slide(planes, amount):
    if amount == 0:
        return planes
    columns = planes.shape[-1]
    rolled = pltpu.roll(planes, amount % columns, axis=1)
    lane = lax.broadcasted_iota(jnp.int32, (planes.shape[0], LANES), 1)
    if amount > 0:
        edge = jnp.where(lane >= amount, rolled[:, :LANES], 0.0)
        return jnp.concatenate([edge, rolled[:, LANES:]], axis=1)
    edge = jnp.where(lane < LANES + amount, rolled[:, columns - LANES :], 0.0)
    return jnp.concatenate([rolled[:, : columns - LANES], edge], axis=1)


def turn(groups, amount, forward):
    lane = lax.broadcasted_iota(jnp.int32, groups[0].shape, 1)
    if forward:
        spun = [pltpu.roll(g, lax.rem(amount, LANES), axis=1) for g in groups]
        return [jnp.where(lane >= amount, g, spun[i - 1]) for i, g in enumerate(spun)]
    spun = [pltpu.roll(g, lax.rem(LANES - amount, LANES), axis=1) for g in groups]
    return [jnp.where(lane < LANES - amount, g, spun[(i + 1) % len(spun)]) for i, g in enumerate(spun)]


def exit_kernel(scale, density_ref, exit_ref):
    slices, cells, columns = density_ref.shape
    count = exit_ref.shape[0]
    amount = slices * (count - 1 - lax.axis_index("light"))
    for index, step in enumerate(STEPS):
        total = jnp.zeros((cells, columns), jnp.float32)
        for k in range(slices):
            total = slide(total + density_ref[k] * scale, step)
        groups = [total[:, g * LANES : (g + 1) * LANES] for g in range(count)]
        if step:
            groups = turn(groups, amount, step > 0)
        for g, values in enumerate(groups):
            exit_ref[g, index * cells : (index + 1) * cells, :] = values


def prefix_kernel(slices, leaving_ref, entering_ref):
    count, planes, _ = leaving_ref.shape
    cells = planes // len(STEPS)
    columns = count * LANES
    place = lax.axis_index("light") * LANES + lax.broadcasted_iota(jnp.int32, (cells, LANES), 1)
    for index, step in enumerate(STEPS):
        part = slice(index * cells, (index + 1) * cells)
        total = jnp.zeros((cells, LANES), jnp.float32)
        for j in range(count):
            entering_ref[j, part, :] = total
            if step and j:
                column = (place - step * slices * (count - 1 - j) + columns) & (columns - 1)
                fresh = column < slices if step > 0 else column >= columns - slices
                total = jnp.where(fresh, 0.0, total)
            total = total + leaving_ref[j, part, :]


def gather_sums(parts, low):
    for bit, mask in enumerate(low):
        merged = []
        for i in range(0, len(parts), 2):
            a, b = parts[i], parts[i + 1]
            merged.append(jnp.where(mask, a, b) + pltpu.roll(jnp.where(mask, b, a), 1 << bit, axis=0))
        parts = merged
    return parts[0]


def brick_kernel(light_scale, view_scale, flip_ref, density_ref, albedo_ref, entering_ref, keep_ref, send_ref, depth_ref, lit_ref):
    slices, cells, columns = density_ref.shape
    count = entering_ref.shape[0]
    core = lax.rem(lax.axis_index("view"), 2)
    light = lax.axis_index("light")
    for index, step in enumerate(STEPS):
        groups = [entering_ref[g, index * cells : (index + 1) * cells, :] for g in range(count)]
        if step:
            groups = turn(groups, slices * (count - light), step < 0)
        for g, values in enumerate(groups):
            depth_ref[index, :, g * LANES : (g + 1) * LANES] = values

    row = lax.broadcasted_iota(jnp.int32, (cells, LANES), 0)
    low = [(row & (1 << bit)) == 0 for bit in range(3)]
    row_wide = lax.broadcasted_iota(jnp.int32, (cells, columns), 0)
    mine_even = core == 0

    def one_slice(k, carry):
        dense = density_ref[k]
        flipped = flip_ref[k] == 1
        depth_view = dense * view_scale
        running = depth_view
        for reach in (1, 2, 4):
            running = running + jnp.where(row_wide >= reach, pltpu.roll(running, reach, axis=0), 0.0)
        total = jnp.broadcast_to(running[cells - 1 :, :], (cells, columns))
        ahead = jnp.where(flipped, total - running, running - depth_view)
        weights = jnp.exp(ahead) * (1.0 - jnp.exp(depth_view))
        dense_light = dense * light_scale
        for index, step in enumerate(STEPS):
            depth = depth_ref[index]
            lit_ref[index] = weights * jnp.exp(depth)
            depth_ref[index] = slide(depth + dense_light, step)
        for pair in range(columns // (8 * LANES)):
            chunks = []
            for chunk in (2 * pair, 2 * pair + 1):
                groups = [slice((4 * chunk + g) * LANES, (4 * chunk + g + 1) * LANES) for g in range(4)]
                reflect = [[albedo_ref[c, k, :, g].astype(jnp.float32) for g in groups] for c in range(3)]
                products = []
                for index in range(len(STEPS)):
                    lit = [lit_ref[index, :, g] for g in groups]
                    for c in range(3):
                        products += [reflect[c][g] * lit[g] for g in range(4)]
                products += [depth_view[:, g] for g in groups]
                tiles = [gather_sums(products[t : t + 8], low) for t in range(0, ROWS, 8)]
                tiles[-1] = jnp.where(low[2], tiles[-1], jnp.exp(jnp.where(low[2], 0.0, tiles[-1])))
                chunks.append(tiles)
            for t, (even, odd) in enumerate(zip(*chunks)):
                keep_ref[pair, k, 8 * t : 8 * t + 8, :] = jnp.where(mine_even, even, odd)
                send_ref[pair, k, 8 * t : 8 * t + 8, :] = jnp.where(mine_even, odd, even)
        return carry

    lax.fori_loop(0, slices, one_slice, 0)


def both_halves(tile, low):
    return jnp.where(low, pltpu.roll(tile, 4, axis=0), tile)


def over(front, back, low):
    through = both_halves(front[-1], low)
    out = [f + through * b for f, b in zip(front[:-1], back[:-1])]
    return out + [jnp.where(low, front[-1], 0.0) + through * back[-1]]


def tiles_of(ref, *index):
    return [ref[(*index, slice(8 * t, 8 * t + 8))] for t in range(ROWS // 8)]


def merge(ref, other_ref, index, other_index, mine_front, low):
    mine, other = tiles_of(ref, *index), tiles_of(other_ref, *other_index)
    front = [jnp.where(mine_front, a, b) for a, b in zip(mine, other)]
    back = [jnp.where(mine_front, b, a) for a, b in zip(mine, other)]
    return over(front, back, low)


def core_kernel(flip_ref, keep_ref, both_ref, out_ref):
    low = lax.broadcasted_iota(jnp.int32, (8, LANES), 0) < 4
    core = lax.rem(lax.axis_index("view"), 2)
    halves, slices = keep_ref.shape[:2]
    for k in range(slices):
        mine_front = core == flip_ref[k]
        for h in range(halves):
            for t, tile in enumerate(merge(keep_ref, both_ref, (h, k), (1 - core, h, k), mine_front, low)):
                out_ref[h, k, 8 * t : 8 * t + 8, :] = tile


def chip_kernel(flip_ref, both_ref, out_ref):
    low = lax.broadcasted_iota(jnp.int32, (8, LANES), 0) < 4
    for k in range(both_ref.shape[1]):
        for t, tile in enumerate(merge(both_ref, both_ref, (0, k), (1, k), flip_ref[k] == 0, low)):
            out_ref[k, 8 * t : 8 * t + 8, :] = tile


def final_kernel(per_slice, flip_ref, shift_ref, color_ref, pieces_ref, out_ref, sums_ref):
    low = lax.broadcasted_iota(jnp.int32, (8, LANES), 0) < 4
    count = pieces_ref.shape[0]
    flipped = flip_ref[lax.axis_index("view") // per_slice] == 1
    current = None
    for j in range(count):
        tiles = tiles_of(pieces_ref, jnp.where(flipped, count - 1 - j, j))
        current = tiles if current is None else over(current, tiles, low)
    for t, tile in enumerate(current):
        sums_ref[8 * t : 8 * t + 8, :] = tile
    for light in range(LIGHTS):
        base = (shift_ref[light] + 1) * 12
        for c in range(3):
            tint = color_ref[light, c]
            for g in range(4):
                out_ref[light, c : c + 1, g * LANES : (g + 1) * LANES] = sums_ref[pl.ds(base + 4 * c + g, 1), :] * tint
        for g in range(4):
            out_ref[light, 3:4, g * LANES : (g + 1) * LANES] = 1.0 - sums_ref[36 + g : 37 + g, :]


def vmem(count):
    return [pl.BlockSpec(memory_space=pltpu.VMEM)] * count


def smem(count):
    return [pl.BlockSpec(memory_space=pltpu.SMEM)] * count


def local(density, albedo, light_color, light_shift, view_flip):
    slices, cells, columns = density.shape
    light_count, view_count = lax.axis_size("light"), lax.axis_size("view")
    light_scale = -LIGHT_DEPTH / (slices * light_count)
    view_scale = -VIEW_DEPTH / (cells * view_count)
    planes = len(STEPS) * cells
    f32 = jnp.float32

    def call(kernel, name, out_shape, in_specs, scratch=()):
        many = isinstance(out_shape, (list, tuple))
        return pl.pallas_call(
            kernel,
            name=name,
            out_shape=out_shape,
            in_specs=in_specs,
            out_specs=vmem(len(out_shape)) if many else vmem(1)[0],
            scratch_shapes=scratch,
            compiler_params=pltpu.CompilerParams(vmem_limit_bytes=16 * 2**20),
        )

    def shaped(*shape):
        return jax.ShapeDtypeStruct(shape, f32)

    lines = shaped(light_count, planes, columns // light_count)
    leaving = call(lambda *refs: exit_kernel(light_scale, *refs), "exits", lines, vmem(1))(density)
    leaving = lax.all_to_all(leaving, "light", 0, 0)
    entering = call(lambda *refs: prefix_kernel(slices, *refs), "prefix", lines, vmem(1))(leaving)
    entering = lax.all_to_all(entering, "light", 0, 0)
    keep, send = call(
        lambda *refs: brick_kernel(light_scale, view_scale, *refs),
        "brick",
        [shaped(2, slices, ROWS, LANES)] * 2,
        smem(1) + vmem(3),
        [pltpu.VMEM((len(STEPS), cells, columns), f32), pltpu.VMEM((len(STEPS), cells, columns), f32)],
    )(view_flip, density, albedo, entering)
    cores = [[2 * z, 2 * z + 1] for z in range(view_count // 2)]
    both = lax.all_gather(send, "view", axis_index_groups=cores)
    merged = call(core_kernel, "cores", shaped(2, slices, ROWS, LANES), smem(1) + vmem(2))(view_flip, keep, both)
    chips = [[v, v + 2] for v in range(view_count) if v & 2 == 0]
    both = lax.all_to_all(merged, "view", 0, 0, axis_index_groups=chips)
    merged = call(chip_kernel, "chips", shaped(slices, ROWS, LANES), smem(1) + vmem(1))(view_flip, both)
    rest = [[4 * k + r for k in range(slices)] for r in range(4)]
    pieces = lax.all_to_all(merged, "view", 0, 0, axis_index_groups=rest)
    return call(
        lambda *refs: final_kernel(view_count // slices, *refs),
        "final",
        shaped(LIGHTS, 4, slices * columns // view_count),
        smem(3) + vmem(1),
        [pltpu.VMEM((ROWS, LANES), f32)],
    )(view_flip, light_shift, light_color, pieces)


def solution(mesh):
    return jax.shard_map(
        local,
        mesh=mesh,
        in_specs=(P("light", "view", None), P(None, "light", "view", None), P(), P(), P("light")),
        out_specs=P(None, None, ("light", "view")),
        check_vma=False,
    )
```

```python
import jax
import jax.numpy as jnp
from jax import lax
from jax.experimental import pallas as pl
from jax.experimental.pallas import tpu as pltpu
from jax.sharding import PartitionSpec as P

LIGHTS = 8
LIGHT_DEPTH = 1.5
VIEW_DEPTH = 2.0
LANES = 128
STEPS = (-1, 0, 1)
ROWS = 40


def slide(planes, amount):
    if amount == 0:
        return planes
    columns = planes.shape[-1]
    rolled = pltpu.roll(planes, amount % columns, axis=1)
    lane = lax.broadcasted_iota(jnp.int32, (planes.shape[0], LANES), 1)
    if amount > 0:
        edge = jnp.where(lane >= amount, rolled[:, :LANES], 0.0)
        return jnp.concatenate([edge, rolled[:, LANES:]], axis=1)
    edge = jnp.where(lane < LANES + amount, rolled[:, columns - LANES :], 0.0)
    return jnp.concatenate([rolled[:, : columns - LANES], edge], axis=1)


def turn(groups, amount, forward):
    lane = lax.broadcasted_iota(jnp.int32, groups[0].shape, 1)
    if forward:
        spun = [pltpu.roll(g, lax.rem(amount, LANES), axis=1) for g in groups]
        return [jnp.where(lane >= amount, g, spun[i - 1]) for i, g in enumerate(spun)]
    spun = [pltpu.roll(g, lax.rem(LANES - amount, LANES), axis=1) for g in groups]
    return [jnp.where(lane < LANES - amount, g, spun[(i + 1) % len(spun)]) for i, g in enumerate(spun)]


def exit_kernel(scale, density_ref, exit_ref, dense_ref, total_ref, arrived):
    slices, cells, columns = density_ref.shape
    count = exit_ref.shape[0]
    copies = [pltpu.make_async_copy(density_ref.at[k], dense_ref.at[k], arrived.at[k]) for k in range(slices)]
    for copy in copies:
        copy.start()
    amount = slices * (count - 1 - lax.axis_index("light"))
    for k in range(slices):
        copies[k].wait()
        dense = dense_ref[k] * scale
        for index, step in enumerate(STEPS):
            total_ref[index] = slide(total_ref[index] + dense if k else dense, step)
    for index, step in enumerate(STEPS):
        total = total_ref[index]
        groups = [total[:, g * LANES : (g + 1) * LANES] for g in range(count)]
        if step:
            groups = turn(groups, amount, step > 0)
        for g, values in enumerate(groups):
            exit_ref[g, index * cells : (index + 1) * cells, :] = values


def prefix_kernel(slices, leaving_ref, entering_ref):
    count, planes, _ = leaving_ref.shape
    cells = planes // len(STEPS)
    columns = count * LANES
    place = lax.axis_index("light") * LANES + lax.broadcasted_iota(jnp.int32, (cells, LANES), 1)
    for index, step in enumerate(STEPS):
        part = slice(index * cells, (index + 1) * cells)
        total = jnp.zeros((cells, LANES), jnp.float32)
        for j in range(count):
            entering_ref[j, part, :] = total
            if step and j:
                column = (place - step * slices * (count - 1 - j) + columns) & (columns - 1)
                fresh = column < slices if step > 0 else column >= columns - slices
                total = jnp.where(fresh, 0.0, total)
            total = total + leaving_ref[j, part, :]


def gather_sums(parts, low):
    for bit, mask in enumerate(low):
        merged = []
        for i in range(0, len(parts), 2):
            a, b = parts[i], parts[i + 1]
            merged.append(jnp.where(mask, a, b) + pltpu.roll(jnp.where(mask, b, a), 1 << bit, axis=0))
        parts = merged
    return parts[0]


def brick_kernel(
    light_scale, view_scale, flip_ref, shift_ref, color_ref, density_ref, albedo_ref, entering_ref, keep_ref, send_ref, depth_ref, lit_ref
):
    slices, cells, columns = density_ref.shape
    count = entering_ref.shape[0]
    core = lax.rem(lax.axis_index("view"), 2)
    light = lax.axis_index("light")
    for index, step in enumerate(STEPS):
        groups = [entering_ref[g, index * cells : (index + 1) * cells, :] for g in range(count)]
        if step:
            groups = turn(groups, slices * (count - light), step < 0)
        for g, values in enumerate(groups):
            depth_ref[index, :, g * LANES : (g + 1) * LANES] = values

    row = lax.broadcasted_iota(jnp.int32, (cells, LANES), 0)
    low = [(row & (1 << bit)) == 0 for bit in range(3)]
    row_wide = lax.broadcasted_iota(jnp.int32, (cells, columns), 0)
    mine_even = core == 0

    def one_slice(k, carry):
        dense = density_ref[k]
        flipped = flip_ref[k] == 1
        depth_view = dense * view_scale
        running = depth_view
        for reach in (1, 2, 4):
            running = running + jnp.where(row_wide >= reach, pltpu.roll(running, reach, axis=0), 0.0)
        total = jnp.broadcast_to(running[cells - 1 :, :], (cells, columns))
        ahead = jnp.where(flipped, total - running, running - depth_view)
        weights = jnp.exp(ahead) * (1.0 - jnp.exp(depth_view))
        dense_light = dense * light_scale
        for index, step in enumerate(STEPS):
            depth = depth_ref[index]
            lit_ref[index] = weights * jnp.exp(depth)
            depth_ref[index] = slide(depth + dense_light, step)
        for pair in range(columns // (8 * LANES)):
            chunks = []
            for chunk in (2 * pair, 2 * pair + 1):
                groups = [slice((4 * chunk + g) * LANES, (4 * chunk + g + 1) * LANES) for g in range(4)]
                reflect = [[albedo_ref[c, k, :, g].astype(jnp.float32) for g in groups] for c in range(3)]
                products = []
                for index in range(len(STEPS)):
                    lit = [lit_ref[index, :, g] for g in groups]
                    for c in range(3):
                        products += [reflect[c][g] * lit[g] for g in range(4)]
                products += [depth_view[:, g] for g in groups]
                tiles = [gather_sums(products[t : t + 8], low) for t in range(0, ROWS, 8)]
                tiles[-1] = jnp.where(low[2], tiles[-1], jnp.exp(jnp.where(low[2], 0.0, tiles[-1])))
                chunks.append(tiles)
            for t, (even, odd) in enumerate(zip(*chunks)):
                keep_ref[pair, k, 8 * t : 8 * t + 8, :] = jnp.where(mine_even, even, odd)
                send_ref[pair, k, 8 * t : 8 * t + 8, :] = jnp.where(mine_even, odd, even)
        return carry

    lax.fori_loop(0, slices, one_slice, 0)


def both_halves(tile, low):
    return jnp.where(low, pltpu.roll(tile, 4, axis=0), tile)


def tiles_of(ref, *index):
    return [ref[(*index, slice(8 * t, 8 * t + 8))] for t in range(ROWS // 8)]


def composite(pieces, low):
    through = None
    for tiles in pieces:
        own = both_halves(tiles[-1], low)
        tiles = tiles[:-1] + [jnp.where(low, tiles[-1], 0.0)]
        if through is None:
            sums, through = tiles, own
        else:
            sums = [total + through * tile for total, tile in zip(sums, tiles)]
            through = through * own
    return sums[:-1] + [jnp.where(low, sums[-1], through)]


def merge(mine, other, mine_front, low):
    front = [jnp.where(mine_front, a, b) for a, b in zip(mine, other)]
    back = [jnp.where(mine_front, b, a) for a, b in zip(mine, other)]
    return composite([front, back], low)


def core_kernel(flip_ref, keep_ref, both_ref, mine_ref, send_ref):
    low = lax.broadcasted_iota(jnp.int32, (8, LANES), 0) < 4
    view = lax.axis_index("view")
    core, chip = view & 1, (view >> 1) & 1
    for k in range(keep_ref.shape[1]):
        mine_front = core == flip_ref[k]
        for half, out_ref in ((chip, mine_ref), (1 - chip, send_ref)):
            merged = merge(tiles_of(keep_ref, half, k), tiles_of(both_ref, 1 - core, half, k), mine_front, low)
            for t, tile in enumerate(merged):
                out_ref[k, 8 * t : 8 * t + 8, :] = tile


def chip_kernel(flip_ref, mine_ref, both_ref, out_ref):
    low = lax.broadcasted_iota(jnp.int32, (8, LANES), 0) < 4
    chip = (lax.axis_index("view") >> 1) & 1
    for k in range(mine_ref.shape[0]):
        merged = merge(tiles_of(mine_ref, k), tiles_of(both_ref, 1 - chip, k), chip == flip_ref[k], low)
        for t, tile in enumerate(merged):
            out_ref[k, 8 * t : 8 * t + 8, :] = tile


def final_kernel(per_slice, flip_ref, shift_ref, color_ref, pieces_ref, out_ref, sums_ref):
    low = lax.broadcasted_iota(jnp.int32, (8, LANES), 0) < 4
    count = pieces_ref.shape[0]
    flipped = flip_ref[lax.axis_index("view") // per_slice] == 1
    order = [jnp.where(flipped, count - 1 - j, j) for j in range(count)]
    for t, tile in enumerate(composite([tiles_of(pieces_ref, j) for j in order], low)):
        sums_ref[8 * t : 8 * t + 8, :] = tile
    for light in range(LIGHTS):
        base = (shift_ref[light] + 1) * 12
        for c in range(3):
            tint = color_ref[c, light]
            for g in range(4):
                out_ref[light, c : c + 1, g * LANES : (g + 1) * LANES] = sums_ref[pl.ds(base + 4 * c + g, 1), :] * tint
        for g in range(4):
            out_ref[light, 3:4, g * LANES : (g + 1) * LANES] = 1.0 - sums_ref[36 + g : 37 + g, :]


def vmem(count):
    return [pl.BlockSpec(memory_space=pltpu.VMEM)] * count


def smem(count):
    return [pl.BlockSpec(memory_space=pltpu.SMEM)] * count


def local(density, albedo, light_color, light_shift, view_flip):
    slices, cells, columns = density.shape
    light_count, view_count = lax.axis_size("light"), lax.axis_size("view")
    light_scale = -LIGHT_DEPTH / (slices * light_count)
    view_scale = -VIEW_DEPTH / (cells * view_count)
    planes = len(STEPS) * cells
    f32 = jnp.float32

    def call(kernel, name, out_shape, in_specs, scratch=()):
        many = isinstance(out_shape, (list, tuple))
        return pl.pallas_call(
            kernel,
            name=name,
            out_shape=out_shape,
            in_specs=in_specs,
            out_specs=vmem(len(out_shape)) if many else vmem(1)[0],
            scratch_shapes=scratch,
            compiler_params=pltpu.CompilerParams(vmem_limit_bytes=16 * 2**20),
        )

    def shaped(*shape):
        return jax.ShapeDtypeStruct(shape, f32)

    lines = shaped(light_count, planes, columns // light_count)
    leaving = call(
        lambda *refs: exit_kernel(light_scale, *refs),
        "exits",
        lines,
        [pl.BlockSpec(memory_space=pltpu.HBM)],
        [
            pltpu.VMEM(density.shape, f32),
            pltpu.VMEM((len(STEPS), cells, columns), f32),
            pltpu.SemaphoreType.DMA((slices,)),
        ],
    )(pltpu.with_memory_space_constraint(density, pltpu.HBM))
    leaving = lax.all_to_all(leaving, "light", 0, 0)
    entering = call(lambda *refs: prefix_kernel(slices, *refs), "prefix", lines, vmem(1))(leaving)
    entering = lax.all_to_all(entering, "light", 0, 0)
    color = light_color.T
    keep, send = call(
        lambda *refs: brick_kernel(light_scale, view_scale, *refs),
        "brick",
        [shaped(2, slices, ROWS, LANES)] * 2,
        smem(3) + vmem(3),
        [pltpu.VMEM((len(STEPS), cells, columns), f32), pltpu.VMEM((len(STEPS), cells, columns), f32)],
    )(view_flip, light_shift, color, density, albedo, entering)
    cores = [[2 * z, 2 * z + 1] for z in range(view_count // 2)]
    both = lax.all_gather(send, "view", axis_index_groups=cores)
    half = shaped(slices, ROWS, LANES)
    mine, send = call(core_kernel, "cores", [half] * 2, smem(1) + vmem(2))(view_flip, keep, both)
    chips = [[v, v + 2] for v in range(view_count) if v & 2 == 0]
    both = lax.all_gather(send, "view", axis_index_groups=chips)
    merged = call(chip_kernel, "chips", half, smem(1) + vmem(2))(view_flip, mine, both)
    rest = [[4 * k + r for k in range(slices)] for r in range(4)]
    pieces = lax.all_to_all(merged, "view", 0, 0, axis_index_groups=rest)
    return call(
        lambda *refs: final_kernel(view_count // slices, *refs),
        "final",
        shaped(LIGHTS, 4, slices * columns // view_count),
        smem(3) + vmem(1),
        [pltpu.VMEM((ROWS, LANES), f32)],
    )(view_flip, light_shift, color, pieces)


def solution(mesh):
    return jax.shard_map(
        local,
        mesh=mesh,
        in_specs=(P("light", "view", None), P(None, "light", "view", None), P(), P(), P("light")),
        out_specs=P(None, None, ("light", "view")),
        check_vma=False,
    )
```

```python
import jax
import jax.numpy as jnp
from jax import lax
from jax.experimental import pallas as pl
from jax.experimental.pallas import tpu as pltpu
from jax.sharding import PartitionSpec as P

LIGHTS = 8
LIGHT_DEPTH = 1.5
VIEW_DEPTH = 2.0
LANES = 128
STEPS = (-1, 0, 1)
ROWS = 40
LIGHT_FIRST = 10
VIEW_FIRST = 5


def slide(planes, amount):
    if amount == 0:
        return planes
    columns = planes.shape[-1]
    rolled = pltpu.roll(planes, amount % columns, axis=1)
    lane = lax.broadcasted_iota(jnp.int32, (planes.shape[0], LANES), 1)
    if amount > 0:
        edge = jnp.where(lane >= amount, rolled[:, :LANES], 0.0)
        return jnp.concatenate([edge, rolled[:, LANES:]], axis=1)
    edge = jnp.where(lane < LANES + amount, rolled[:, columns - LANES :], 0.0)
    return jnp.concatenate([rolled[:, : columns - LANES], edge], axis=1)


def turn(groups, amount, forward):
    lane = lax.broadcasted_iota(jnp.int32, groups[0].shape, 1)
    if forward:
        spun = [pltpu.roll(g, lax.rem(amount, LANES), axis=1) for g in groups]
        return [jnp.where(lane >= amount, g, spun[i - 1]) for i, g in enumerate(spun)]
    spun = [pltpu.roll(g, lax.rem(LANES - amount, LANES), axis=1) for g in groups]
    return [jnp.where(lane < LANES - amount, g, spun[(i + 1) % len(spun)]) for i, g in enumerate(spun)]


def exit_kernel(scale, density_ref, exit_ref, dense_ref, total_ref, arrived):
    slices, cells, columns = density_ref.shape
    count = exit_ref.shape[0]
    copies = [pltpu.make_async_copy(density_ref.at[k], dense_ref.at[k], arrived.at[k]) for k in range(slices)]
    for copy in copies:
        copy.start()
    amount = slices * (count - 1 - lax.axis_index("light"))
    for k in range(slices):
        copies[k].wait()
        dense = dense_ref[k] * scale
        for index, step in enumerate(STEPS):
            total_ref[index] = slide(total_ref[index] + dense if k else dense, step)
    for index, step in enumerate(STEPS):
        total = total_ref[index]
        groups = [total[:, g * LANES : (g + 1) * LANES] for g in range(count)]
        if step:
            groups = turn(groups, amount, step > 0)
        for g, values in enumerate(groups):
            exit_ref[g, index * cells : (index + 1) * cells, :] = values


def prefix_kernel(slices, leaving_ref, entering_ref):
    count, planes, _ = leaving_ref.shape
    cells = planes // len(STEPS)
    columns = count * LANES
    position = lax.rem(lax.axis_index("light") + count - LIGHT_FIRST, count)
    place = position * LANES + lax.broadcasted_iota(jnp.int32, (cells, LANES), 1)
    for index, step in enumerate(STEPS):
        part = slice(index * cells, (index + 1) * cells)
        total = jnp.zeros((cells, LANES), jnp.float32)
        for j in range(count):
            member = (j - LIGHT_FIRST) % count
            entering_ref[member, part, :] = total
            if step and j:
                column = (place - step * slices * (count - 1 - j) + columns) & (columns - 1)
                fresh = column < slices if step > 0 else column >= columns - slices
                total = jnp.where(fresh, 0.0, total)
            total = total + leaving_ref[member, part, :]


def gather_sums(parts, low):
    for bit, mask in enumerate(low):
        merged = []
        for i in range(0, len(parts), 2):
            a, b = parts[i], parts[i + 1]
            merged.append(jnp.where(mask, a, b) + pltpu.roll(jnp.where(mask, b, a), 1 << bit, axis=0))
        parts = merged
    return parts[0]


def brick_kernel(
    light_scale, view_scale, flip_ref, shift_ref, color_ref, density_ref, albedo_ref, entering_ref, keep_ref, send_ref, depth_ref, lit_ref
):
    slices, cells, columns = density_ref.shape
    count = entering_ref.shape[0]
    core = lax.rem(lax.axis_index("view"), 2)
    light = lax.axis_index("light")
    for index, step in enumerate(STEPS):
        groups = [entering_ref[g, index * cells : (index + 1) * cells, :] for g in range(count)]
        if step:
            groups = turn(groups, slices * (count - light), step < 0)
        for g, values in enumerate(groups):
            depth_ref[index, :, g * LANES : (g + 1) * LANES] = values

    row = lax.broadcasted_iota(jnp.int32, (cells, LANES), 0)
    low = [(row & (1 << bit)) == 0 for bit in range(3)]
    row_wide = lax.broadcasted_iota(jnp.int32, (cells, columns), 0)
    mine_even = core == 0

    def one_slice(k, carry):
        dense = density_ref[k]
        flipped = flip_ref[k] == 1
        depth_view = dense * view_scale
        running = depth_view
        for reach in (1, 2, 4):
            running = running + jnp.where(row_wide >= reach, pltpu.roll(running, reach, axis=0), 0.0)
        total = jnp.broadcast_to(running[cells - 1 :, :], (cells, columns))
        ahead = jnp.where(flipped, total - running, running - depth_view)
        weights = jnp.exp(ahead) * (1.0 - jnp.exp(depth_view))
        dense_light = dense * light_scale
        for index, step in enumerate(STEPS):
            depth = depth_ref[index]
            lit_ref[index] = weights * jnp.exp(depth)
            depth_ref[index] = slide(depth + dense_light, step)
        for pair in range(columns // (8 * LANES)):
            chunks = []
            for chunk in (2 * pair, 2 * pair + 1):
                groups = [slice((4 * chunk + g) * LANES, (4 * chunk + g + 1) * LANES) for g in range(4)]
                reflect = [[albedo_ref[c, k, :, g].astype(jnp.float32) for g in groups] for c in range(3)]
                products = []
                for index in range(len(STEPS)):
                    lit = [lit_ref[index, :, g] for g in groups]
                    for c in range(3):
                        products += [reflect[c][g] * lit[g] for g in range(4)]
                products += [depth_view[:, g] for g in groups]
                tiles = [gather_sums(products[t : t + 8], low) for t in range(0, ROWS, 8)]
                tiles[-1] = jnp.where(low[2], tiles[-1], jnp.exp(jnp.where(low[2], 0.0, tiles[-1])))
                chunks.append(tiles)
            for t, (even, odd) in enumerate(zip(*chunks)):
                keep_ref[pair, k, 8 * t : 8 * t + 8, :] = jnp.where(mine_even, even, odd)
                send_ref[pair, k, 8 * t : 8 * t + 8, :] = jnp.where(mine_even, odd, even)
        return carry

    lax.fori_loop(0, slices, one_slice, 0)


def both_halves(tile, low):
    return jnp.where(low, pltpu.roll(tile, 4, axis=0), tile)


def tiles_of(ref, *index):
    return [ref[(*index, slice(8 * t, 8 * t + 8))] for t in range(ROWS // 8)]


def composite(pieces, low):
    through = None
    for tiles in pieces:
        own = both_halves(tiles[-1], low)
        tiles = tiles[:-1] + [jnp.where(low, tiles[-1], 0.0)]
        if through is None:
            sums, through = tiles, own
        else:
            sums = [total + through * tile for total, tile in zip(sums, tiles)]
            through = through * own
    return sums[:-1] + [jnp.where(low, sums[-1], through)]


def merge(mine, other, mine_front, low):
    front = [jnp.where(mine_front, a, b) for a, b in zip(mine, other)]
    back = [jnp.where(mine_front, b, a) for a, b in zip(mine, other)]
    return composite([front, back], low)


def core_kernel(flip_ref, keep_ref, both_ref, mine_ref, send_ref):
    low = lax.broadcasted_iota(jnp.int32, (8, LANES), 0) < 4
    view = lax.axis_index("view")
    core, chip = view & 1, (view >> 1) & 1
    for k in range(keep_ref.shape[1]):
        mine_front = core == flip_ref[k]
        for half, out_ref in ((chip, mine_ref), (1 - chip, send_ref)):
            merged = merge(tiles_of(keep_ref, half, k), tiles_of(both_ref, 1 - core, half, k), mine_front, low)
            for t, tile in enumerate(merged):
                out_ref[k, 8 * t : 8 * t + 8, :] = tile


def chip_kernel(flip_ref, mine_ref, both_ref, out_ref):
    low = lax.broadcasted_iota(jnp.int32, (8, LANES), 0) < 4
    chip = (lax.axis_index("view") >> 1) & 1
    for k in range(mine_ref.shape[0]):
        merged = merge(tiles_of(mine_ref, k), tiles_of(both_ref, 1 - chip, k), chip == flip_ref[k], low)
        for t, tile in enumerate(merged):
            out_ref[(k - VIEW_FIRST) % mine_ref.shape[0], 8 * t : 8 * t + 8, :] = tile


def final_kernel(per_slice, flip_ref, shift_ref, color_ref, pieces_ref, out_ref, sums_ref):
    low = lax.broadcasted_iota(jnp.int32, (8, LANES), 0) < 4
    count = pieces_ref.shape[0]
    flipped = flip_ref[lax.axis_index("view") // per_slice] == 1
    order = [jnp.where(flipped, (count - 1 - j - VIEW_FIRST) % count, (j - VIEW_FIRST) % count) for j in range(count)]
    for t, tile in enumerate(composite([tiles_of(pieces_ref, j) for j in order], low)):
        sums_ref[8 * t : 8 * t + 8, :] = tile
    for light in range(LIGHTS):
        base = (shift_ref[light] + 1) * 12
        for c in range(3):
            tint = color_ref[c, light]
            for g in range(4):
                out_ref[light, c : c + 1, g * LANES : (g + 1) * LANES] = sums_ref[pl.ds(base + 4 * c + g, 1), :] * tint
        for g in range(4):
            out_ref[light, 3:4, g * LANES : (g + 1) * LANES] = 1.0 - sums_ref[36 + g : 37 + g, :]


def vmem(count):
    return [pl.BlockSpec(memory_space=pltpu.VMEM)] * count


def smem(count):
    return [pl.BlockSpec(memory_space=pltpu.SMEM)] * count


def local(density, albedo, light_color, light_shift, view_flip):
    slices, cells, columns = density.shape
    light_count, view_count = lax.axis_size("light"), lax.axis_size("view")
    light_scale = -LIGHT_DEPTH / (slices * light_count)
    view_scale = -VIEW_DEPTH / (cells * view_count)
    planes = len(STEPS) * cells
    f32 = jnp.float32

    def call(kernel, name, out_shape, in_specs, scratch=()):
        many = isinstance(out_shape, (list, tuple))
        return pl.pallas_call(
            kernel,
            name=name,
            out_shape=out_shape,
            in_specs=in_specs,
            out_specs=vmem(len(out_shape)) if many else vmem(1)[0],
            scratch_shapes=scratch,
            compiler_params=pltpu.CompilerParams(vmem_limit_bytes=16 * 2**20),
        )

    def shaped(*shape):
        return jax.ShapeDtypeStruct(shape, f32)

    lines = shaped(light_count, planes, columns // light_count)
    leaving = call(
        lambda *refs: exit_kernel(light_scale, *refs),
        "exits",
        lines,
        [pl.BlockSpec(memory_space=pltpu.HBM)],
        [
            pltpu.VMEM(density.shape, f32),
            pltpu.VMEM((len(STEPS), cells, columns), f32),
            pltpu.SemaphoreType.DMA((slices,)),
        ],
    )(pltpu.with_memory_space_constraint(density, pltpu.HBM))
    along = [[(j + LIGHT_FIRST) % light_count for j in range(light_count)]]
    leaving = lax.all_to_all(leaving, "light", 0, 0, axis_index_groups=along)
    entering = call(lambda *refs: prefix_kernel(slices, *refs), "prefix", lines, vmem(1))(leaving)
    entering = lax.all_to_all(entering, "light", 0, 0, axis_index_groups=along)
    color = light_color.T
    keep, send = call(
        lambda *refs: brick_kernel(light_scale, view_scale, *refs),
        "brick",
        [shaped(2, slices, ROWS, LANES)] * 2,
        smem(3) + vmem(3),
        [pltpu.VMEM((len(STEPS), cells, columns), f32), pltpu.VMEM((len(STEPS), cells, columns), f32)],
    )(view_flip, light_shift, color, density, albedo, entering)
    cores = [[2 * z, 2 * z + 1] for z in range(view_count // 2)]
    both = lax.all_gather(send, "view", axis_index_groups=cores)
    half = shaped(slices, ROWS, LANES)
    mine, send = call(core_kernel, "cores", [half] * 2, smem(1) + vmem(2))(view_flip, keep, both)
    chips = [[v, v + 2] for v in range(view_count) if v & 2 == 0]
    both = lax.all_gather(send, "view", axis_index_groups=chips)
    merged = call(chip_kernel, "chips", half, smem(1) + vmem(2))(view_flip, mine, both)
    rest = [[4 * ((k + VIEW_FIRST) % slices) + r for k in range(slices)] for r in range(4)]
    pieces = lax.all_to_all(merged, "view", 0, 0, axis_index_groups=rest)
    return call(
        lambda *refs: final_kernel(view_count // slices, *refs),
        "final",
        shaped(LIGHTS, 4, slices * columns // view_count),
        smem(3) + vmem(1),
        [pltpu.VMEM((ROWS, LANES), f32)],
    )(view_flip, light_shift, color, pieces)


def solution(mesh):
    return jax.shard_map(
        local,
        mesh=mesh,
        in_specs=(P("light", "view", None), P(None, "light", "view", None), P(), P(), P("light")),
        out_specs=P(None, None, ("light", "view")),
        check_vma=False,
    )
```

```python
import jax
import jax.numpy as jnp
from jax import lax
from jax.experimental import pallas as pl
from jax.experimental.pallas import tpu as pltpu
from jax.sharding import PartitionSpec as P

LIGHTS = 8
LIGHT_DEPTH = 1.5
VIEW_DEPTH = 2.0
LANES = 128
STEPS = (-1, 0, 1)
CHANNELS = ((0, 0), (0, 1), (1, 0), (1, 1), (2, 0), (2, 1), (0, 2), (1, 2), (2, 2))
ROWS = 40
LIGHT_ORDER = (10, 9, 8, 7, 6, 5, 4, 3, 2, 1, 0, 15, 14, 13, 12, 11)
VIEW_ORDER = (5, 1, 3, 7, 4, 0, 2, 6)
PARTS = 2


def slide(planes, amount):
    if amount == 0:
        return planes
    columns = planes.shape[-1]
    rolled = pltpu.roll(planes, amount % columns, axis=1)
    lane = lax.broadcasted_iota(jnp.int32, (planes.shape[0], LANES), 1)
    if amount > 0:
        edge = jnp.where(lane >= amount, rolled[:, :LANES], 0.0)
        return jnp.concatenate([edge, rolled[:, LANES:]], axis=1)
    edge = jnp.where(lane < LANES + amount, rolled[:, columns - LANES :], 0.0)
    return jnp.concatenate([rolled[:, : columns - LANES], edge], axis=1)


def turn(groups, amount, forward):
    lane = lax.broadcasted_iota(jnp.int32, groups[0].shape, 1)
    if forward:
        spun = [pltpu.roll(g, lax.rem(amount, LANES), axis=1) for g in groups]
        return [jnp.where(lane >= amount, g, spun[i - 1]) for i, g in enumerate(spun)]
    spun = [pltpu.roll(g, lax.rem(LANES - amount, LANES), axis=1) for g in groups]
    return [jnp.where(lane < LANES - amount, g, spun[(i + 1) % len(spun)]) for i, g in enumerate(spun)]


def exit_kernel(scale, density_ref, exit_ref, dense_ref, total_ref, arrived):
    slices, cells, columns = density_ref.shape
    count = exit_ref.shape[0]
    size = slices // PARTS
    copies = []
    for part in range(PARTS):
        span = pl.ds(part * size, size)
        copies.append(pltpu.make_async_copy(density_ref.at[span], dense_ref.at[span], arrived.at[part]))
        copies[-1].start()
    amount = slices * (count - 1 - lax.axis_index("light"))
    for part, copy in enumerate(copies):
        copy.wait()
        for index, step in enumerate(STEPS):
            sums = [dense_ref[k] * scale for k in range(part * size, part * size + size)]
            reach = 1
            while len(sums) > 1:
                sums = [slide(a, reach * step) + b for a, b in zip(sums[::2], sums[1::2])]
                reach *= 2
            total_ref[index] = slide(total_ref[index], size * step) + sums[0] if part else sums[0]
    for index, step in enumerate(STEPS):
        total = slide(total_ref[index], step)
        groups = [total[:, g * LANES : (g + 1) * LANES] for g in range(count)]
        if step:
            groups = turn(groups, amount, step > 0)
        for g, values in enumerate(groups):
            exit_ref[g, index * cells : (index + 1) * cells, :] = values


def spread(ref, row, column):
    return jnp.broadcast_to(ref[row : row + 1, column : column + 1], (8, LANES))


def prefix_kernel(slices, leaving_ref, flip_ref, shift_ref, color_ref, entering_ref, flips_ref):
    for k in range(slices):
        flips_ref[k] = spread(flip_ref, 0, k)
    count, planes, _ = leaving_ref.shape
    cells = planes // len(STEPS)
    columns = count * LANES
    light = lax.axis_index("light")
    position = sum(jnp.where(light == member, p, 0) for p, member in enumerate(LIGHT_ORDER))
    place = position * LANES + lax.broadcasted_iota(jnp.int32, (cells, LANES), 1)
    for index, step in enumerate(STEPS):
        part = slice(index * cells, (index + 1) * cells)
        total = jnp.zeros((cells, LANES), jnp.float32)
        for j in range(count):
            member = LIGHT_ORDER.index(j)
            entering_ref[member, part, :] = total
            if step and j:
                column = (place - step * slices * (count - 1 - j) + columns) & (columns - 1)
                fresh = column < slices if step > 0 else column >= columns - slices
                total = jnp.where(fresh, 0.0, total)
            total = total + leaving_ref[member, part, :]


def gather_sums(parts, low):
    for bit, mask in enumerate(low):
        merged = []
        for i in range(0, len(parts), 2):
            a, b = parts[i], parts[i + 1]
            merged.append(jnp.where(mask, a, b) + pltpu.roll(jnp.where(mask, b, a), 1 << bit, axis=0))
        parts = merged
    return parts[0]


def brick_kernel(
    light_scale, view_scale, flips_ref, density_ref, albedo_ref, entering_ref, keep_ref, send_ref, depth_ref, lit_ref
):
    slices, cells, columns = density_ref.shape
    count = entering_ref.shape[0]
    core = lax.rem(lax.axis_index("view"), 2)
    light = lax.axis_index("light")
    for index, step in enumerate(STEPS):
        groups = [entering_ref[g, index * cells : (index + 1) * cells, :] for g in range(count)]
        if step:
            groups = turn(groups, slices * (count - light), step < 0)
        for g, values in enumerate(groups):
            depth_ref[index, :, g * LANES : (g + 1) * LANES] = values

    row = lax.broadcasted_iota(jnp.int32, (cells, LANES), 0)
    low = [(row & (1 << bit)) == 0 for bit in range(3)]
    row_wide = lax.broadcasted_iota(jnp.int32, (cells, columns), 0)
    mine_even = core == 0

    def one_slice(k, carry):
        dense = density_ref[k]
        flipped = jnp.concatenate([flips_ref[k]] * (columns // LANES), axis=1) == 1
        depth_view = dense * view_scale
        running = depth_view
        for reach in (1, 2, 4):
            running = running + jnp.where(row_wide >= reach, pltpu.roll(running, reach, axis=0), 0.0)
        total = jnp.broadcast_to(running[cells - 1 :, :], (cells, columns))
        ahead = jnp.where(flipped, total - running, running - depth_view)
        weights = jnp.exp(ahead) * (1.0 - jnp.exp(depth_view))
        dense_light = dense * light_scale
        for index, step in enumerate(STEPS):
            depth = depth_ref[index]
            lit_ref[index] = weights * jnp.exp(depth)
            depth_ref[index] = slide(depth + dense_light, step)
        for pair in range(columns // (8 * LANES)):
            chunks = []
            for chunk in (2 * pair, 2 * pair + 1):
                groups = [slice((4 * chunk + g) * LANES, (4 * chunk + g + 1) * LANES) for g in range(4)]
                reflect = [[albedo_ref[c, k, :, g].astype(jnp.float32) for g in groups] for c in range(3)]
                lit = [[lit_ref[index, :, g] for g in groups] for index in range(len(STEPS))]
                products = []
                for index, c in CHANNELS:
                    products += [reflect[c][g] * lit[index][g] for g in range(4)]
                products += [depth_view[:, g] for g in groups]
                tiles = [gather_sums(products[t : t + 8], low) for t in range(0, ROWS, 8)]
                tiles[-1] = jnp.where(low[2], tiles[-1], jnp.exp(jnp.where(low[2], 0.0, tiles[-1])))
                chunks.append(tiles)
            for t, (even, odd) in enumerate(zip(*chunks)):
                keep_ref[pair, k, 8 * t : 8 * t + 8, :] = jnp.where(mine_even, even, odd)
                send_ref[pair, k, 8 * t : 8 * t + 8, :] = jnp.where(mine_even, odd, even)
        return carry

    lax.fori_loop(0, slices, one_slice, 0)


def both_halves(tile, low):
    return jnp.where(low, pltpu.roll(tile, 4, axis=0), tile)


def tiles_of(ref, *index):
    return [ref[(*index, slice(8 * t, 8 * t + 8))] for t in range(ROWS // 8)]


def composite(pieces, low):
    through = None
    for tiles in pieces:
        own = both_halves(tiles[-1], low)
        tiles = tiles[:-1] + [jnp.where(low, tiles[-1], 0.0)]
        if through is None:
            sums, through = tiles, own
        else:
            sums = [total + through * tile for total, tile in zip(sums, tiles)]
            through = through * own
    return sums[:-1] + [jnp.where(low, sums[-1], through)]


def merge(mine, other, mine_front, low):
    front = [jnp.where(mine_front, a, b) for a, b in zip(mine, other)]
    back = [jnp.where(mine_front, b, a) for a, b in zip(mine, other)]
    return composite([front, back], low)


def core_kernel(flips_ref, keep_ref, both_ref, mine_ref, send_ref):
    low = lax.broadcasted_iota(jnp.int32, (8, LANES), 0) < 4
    view = lax.axis_index("view")
    core, chip = view & 1, (view >> 1) & 1
    for k in range(keep_ref.shape[1]):
        mine_front = flips_ref[k] == core
        for half, out_ref in ((chip, mine_ref), (1 - chip, send_ref)):
            merged = merge(tiles_of(keep_ref, half, k), tiles_of(both_ref, 1 - core, half, k), mine_front, low)
            for t, tile in enumerate(merged):
                out_ref[k, 8 * t : 8 * t + 8, :] = tile


def chip_kernel(flips_ref, mine_ref, both_ref, out_ref):
    low = lax.broadcasted_iota(jnp.int32, (8, LANES), 0) < 4
    chip = (lax.axis_index("view") >> 1) & 1
    for k in range(mine_ref.shape[0]):
        merged = merge(tiles_of(mine_ref, k), tiles_of(both_ref, 1 - chip, k), flips_ref[k] == chip, low)
        for t, tile in enumerate(merged):
            out_ref[VIEW_ORDER.index(k), 8 * t : 8 * t + 8, :] = tile


def final_kernel(per_slice, flips_ref, shift_ref, color_ref, pieces_ref, out_ref, rows_ref):
    low = lax.broadcasted_iota(jnp.int32, (8, LANES), 0) < 4
    count = pieces_ref.shape[0]
    flipped = flips_ref[lax.axis_index("view") // per_slice] == 1
    ordered = []
    for j in range(count):
        near, far = tiles_of(pieces_ref, VIEW_ORDER.index(j)), tiles_of(pieces_ref, VIEW_ORDER.index(count - 1 - j))
        ordered.append([jnp.where(flipped, b, a) for a, b in zip(near, far)])
    first, second, third, blue, last = composite(ordered, low)
    blue_second = pltpu.roll(blue, 4, axis=0)
    opacity = 1.0 - last
    for light in range(LIGHTS):
        step = spread(shift_ref, 0, light)
        red_green = jnp.where(step == 0, second, jnp.where(step < 0, first, third))
        blues = jnp.where(step == 0, blue_second, jnp.where(step < 0, blue, last))
        tint = [spread(color_ref, c, light) for c in range(3)]
        rows_ref[light, 0:8, :] = red_green * jnp.where(low, tint[0], tint[1])
        rows_ref[light, 8:16, :] = jnp.where(low, blues * tint[2], opacity)
    for light in range(LIGHTS):
        for g in range(4):
            out_ref[light, :, g * LANES : (g + 1) * LANES] = rows_ref[light, pl.ds(g, 4, stride=4), :]


def vmem(count):
    return [pl.BlockSpec(memory_space=pltpu.VMEM)] * count


def local(density, albedo, light_color, light_shift, view_flip):
    slices, cells, columns = density.shape
    light_count, view_count = lax.axis_size("light"), lax.axis_size("view")
    light_scale = -LIGHT_DEPTH / (slices * light_count)
    view_scale = -VIEW_DEPTH / (cells * view_count)
    planes = len(STEPS) * cells
    f32 = jnp.float32

    def call(kernel, name, out_shape, in_specs, scratch=()):
        many = isinstance(out_shape, (list, tuple))
        return pl.pallas_call(
            kernel,
            name=name,
            out_shape=out_shape,
            in_specs=in_specs,
            out_specs=vmem(len(out_shape)) if many else vmem(1)[0],
            scratch_shapes=scratch,
            compiler_params=pltpu.CompilerParams(vmem_limit_bytes=16 * 2**20),
        )

    def shaped(*shape, kind=f32):
        return jax.ShapeDtypeStruct(shape, kind)

    lines = shaped(light_count, planes, columns // light_count)
    leaving = call(
        lambda *refs: exit_kernel(light_scale, *refs),
        "exits",
        lines,
        [pl.BlockSpec(memory_space=pltpu.HBM)],
        [
            pltpu.VMEM(density.shape, f32),
            pltpu.VMEM((len(STEPS), cells, columns), f32),
            pltpu.SemaphoreType.DMA((PARTS,)),
        ],
    )(pltpu.with_memory_space_constraint(density, pltpu.HBM))
    leaving, albedo = lax.optimization_barrier((leaving, albedo))
    along = [list(LIGHT_ORDER)]
    leaving = lax.all_to_all(leaving, "light", 0, 0, axis_index_groups=along)
    flip, shift, color = view_flip.reshape(1, -1), light_shift.reshape(1, -1), light_color.T
    entering, flips = call(
        lambda *refs: prefix_kernel(slices, *refs), "prefix", [lines, shaped(slices, 8, LANES, kind=jnp.int32)], vmem(4)
    )(leaving, flip, shift, color)
    entering = lax.all_to_all(entering, "light", 0, 0, axis_index_groups=along)
    keep, send = call(
        lambda *refs: brick_kernel(light_scale, view_scale, *refs),
        "brick",
        [shaped(2, slices, ROWS, LANES)] * 2,
        vmem(4),
        [pltpu.VMEM((len(STEPS), cells, columns), f32), pltpu.VMEM((len(STEPS), cells, columns), f32)],
    )(flips, density, albedo, entering)
    cores = [[2 * z, 2 * z + 1] for z in range(view_count // 2)]
    both = lax.all_gather(send, "view", axis_index_groups=cores)
    half = shaped(slices, ROWS, LANES)
    mine, send = call(core_kernel, "cores", [half] * 2, vmem(3))(flips, keep, both)
    chips = [[v, v + 2] for v in range(view_count) if v & 2 == 0]
    both = lax.all_gather(send, "view", axis_index_groups=chips)
    merged = call(chip_kernel, "chips", half, vmem(3))(flips, mine, both)
    rest = [[4 * k + r for k in VIEW_ORDER] for r in range(4)]
    pieces = lax.all_to_all(merged, "view", 0, 0, axis_index_groups=rest)
    return call(
        lambda *refs: final_kernel(view_count // slices, *refs),
        "final",
        shaped(LIGHTS, 4, slices * columns // view_count),
        vmem(4),
        [pltpu.VMEM((LIGHTS, 16, LANES), f32)],
    )(flips, shift, color, pieces)


def solution(mesh):
    return jax.shard_map(
        local,
        mesh=mesh,
        in_specs=(P("light", "view", None), P(None, "light", "view", None), P(), P(), P("light")),
        out_specs=P(None, None, ("light", "view")),
        check_vma=False,
    )
```

```python
import math

import jax
import jax.numpy as jnp
from jax import lax
from jax.experimental import pallas as pl
from jax.experimental.pallas import tpu as pltpu
from jax.sharding import PartitionSpec as P

LIGHTS = 8
LIGHT_DEPTH = 1.5
VIEW_DEPTH = 2.0
LANES = 128
STEPS = (-1, 0, 1)
CHANNELS = ((0, 0), (0, 1), (1, 0), (1, 1), (2, 0), (2, 1), (0, 2), (1, 2), (2, 2))
ROWS = 40
LIGHT_ORDER = (10, 9, 8, 7, 6, 5, 4, 3, 2, 1, 0, 15, 14, 13, 12, 11)
VIEW_ORDER = (5, 1, 3, 7, 0, 4, 2, 6)
PARTS = 2


def slide(planes, amount):
    if amount == 0:
        return planes
    columns = planes.shape[-1]
    rolled = pltpu.roll(planes, amount % columns, axis=1)
    lane = lax.broadcasted_iota(jnp.int32, (planes.shape[0], LANES), 1)
    if amount > 0:
        edge = jnp.where(lane >= amount, rolled[:, :LANES], 0.0)
        return jnp.concatenate([edge, rolled[:, LANES:]], axis=1)
    edge = jnp.where(lane < LANES + amount, rolled[:, columns - LANES :], 0.0)
    return jnp.concatenate([rolled[:, : columns - LANES], edge], axis=1)


def turn(groups, amount, forward):
    lane = lax.broadcasted_iota(jnp.int32, groups[0].shape, 1)
    if forward:
        spun = [pltpu.roll(g, lax.rem(amount, LANES), axis=1) for g in groups]
        return [jnp.where(lane >= amount, g, spun[i - 1]) for i, g in enumerate(spun)]
    spun = [pltpu.roll(g, lax.rem(LANES - amount, LANES), axis=1) for g in groups]
    return [jnp.where(lane < LANES - amount, g, spun[(i + 1) % len(spun)]) for i, g in enumerate(spun)]


def exit_kernel(scale, density_ref, exit_ref, dense_ref, total_ref, arrived):
    slices, cells, columns = density_ref.shape
    count = exit_ref.shape[0]
    size = slices // PARTS
    copies = []
    for part in range(PARTS):
        span = pl.ds(part * size, size)
        copies.append(pltpu.make_async_copy(density_ref.at[span], dense_ref.at[span], arrived.at[part]))
        copies[-1].start()
    amount = slices * (count - 1 - lax.axis_index("light"))
    for part, copy in enumerate(copies):
        copy.wait()
        for index, step in enumerate(STEPS):
            sums = [dense_ref[k] * scale for k in range(part * size, part * size + size)]
            reach = 1
            while len(sums) > 1:
                sums = [slide(a, reach * step) + b for a, b in zip(sums[::2], sums[1::2])]
                reach *= 2
            total_ref[index] = slide(total_ref[index], size * step) + sums[0] if part else sums[0]
    for index, step in enumerate(STEPS):
        total = slide(total_ref[index], step)
        groups = [total[:, g * LANES : (g + 1) * LANES] for g in range(count)]
        if step:
            groups = turn(groups, amount, step > 0)
        for g, values in enumerate(groups):
            exit_ref[g, index * cells : (index + 1) * cells, :] = values


def spread(ref, row, column):
    return jnp.broadcast_to(ref[row : row + 1, column : column + 1], (8, LANES))


def prefix_kernel(slices, leaving_ref, flip_ref, shift_ref, color_ref, entering_ref, flips_ref):
    for k in range(slices):
        flips_ref[k] = spread(flip_ref, 0, k)
    count, planes, _ = leaving_ref.shape
    cells = planes // len(STEPS)
    columns = count * LANES
    light = lax.axis_index("light")
    position = sum(jnp.where(light == member, p, 0) for p, member in enumerate(LIGHT_ORDER))
    place = position * LANES + lax.broadcasted_iota(jnp.int32, (cells, LANES), 1)
    for index, step in enumerate(STEPS):
        part = slice(index * cells, (index + 1) * cells)
        total = jnp.zeros((cells, LANES), jnp.float32)
        for j in range(count):
            member = LIGHT_ORDER.index(j)
            entering_ref[member, part, :] = total
            if step and j:
                column = (place - step * slices * (count - 1 - j) + columns) & (columns - 1)
                fresh = column < slices if step > 0 else column >= columns - slices
                total = jnp.where(fresh, 0.0, total)
            total = total + leaving_ref[member, part, :]


def gather_sums(parts, ref, base):
    for r, part in enumerate(parts):
        ref[base + 8 * r : base + 8 * r + 8, :] = part
    rows = [ref[pl.ds(base + y, 8, stride=8), :] for y in range(8)]
    while len(rows) > 1:
        rows = [a + b for a, b in zip(rows[::2], rows[1::2])]
    return rows[0]


def brick_kernel(
    light_scale, view_scale, flips_ref, density_ref, albedo_ref, entering_ref, keep_ref, send_ref, depth_ref, lit_ref, turn_ref
):
    slices, cells, columns = density_ref.shape
    count = entering_ref.shape[0]
    core = lax.rem(lax.axis_index("view"), 2)
    light = lax.axis_index("light")
    for index, step in enumerate(STEPS):
        groups = [entering_ref[g, index * cells : (index + 1) * cells, :] for g in range(count)]
        if step:
            groups = turn(groups, slices * (count - light), step < 0)
        for g, values in enumerate(groups):
            depth_ref[index, :, g * LANES : (g + 1) * LANES] = values

    low = lax.broadcasted_iota(jnp.int32, (cells, LANES), 0) < 4
    row_wide = lax.broadcasted_iota(jnp.int32, (cells, columns), 0)
    mine_even = core == 0

    def one_slice(k, carry):
        dense = density_ref[k]
        flipped = jnp.concatenate([flips_ref[k]] * (columns // LANES), axis=1) == 1
        depth_view = dense * view_scale
        running = depth_view
        for reach in (1, 2, 4):
            running = running + jnp.where(row_wide >= reach, pltpu.roll(running, reach, axis=0), 0.0)
        total = jnp.broadcast_to(running[cells - 1 :, :], (cells, columns))
        ahead = jnp.where(flipped, total - running, running - depth_view)
        weights = jnp.exp2(ahead) * (1.0 - jnp.exp2(depth_view))
        dense_light = dense * light_scale
        for index, step in enumerate(STEPS):
            depth = depth_ref[index]
            lit_ref[index] = weights * jnp.exp2(depth)
            depth_ref[index] = slide(depth + dense_light, step)
        for pair in range(columns // (8 * LANES)):
            chunks = []
            for chunk in (2 * pair, 2 * pair + 1):
                groups = [slice((4 * chunk + g) * LANES, (4 * chunk + g + 1) * LANES) for g in range(4)]
                reflect = [[albedo_ref[c, k, :, g].astype(jnp.float32) for g in groups] for c in range(3)]
                lit = [[lit_ref[index, :, g] for g in groups] for index in range(len(STEPS))]
                products = []
                for index, c in CHANNELS:
                    products += [reflect[c][g] * lit[index][g] for g in range(4)]
                products += [depth_view[:, g] for g in groups]
                tiles = [gather_sums(products[t : t + 8], turn_ref, 8 * (chunk * ROWS + t)) for t in range(0, ROWS, 8)]
                tiles[-1] = jnp.where(low, tiles[-1], jnp.exp2(jnp.where(low, 0.0, tiles[-1])))
                chunks.append(tiles)
            for t, (even, odd) in enumerate(zip(*chunks)):
                keep_ref[pair, k, 8 * t : 8 * t + 8, :] = jnp.where(mine_even, even, odd)
                send_ref[pair, k, 8 * t : 8 * t + 8, :] = jnp.where(mine_even, odd, even)
        return carry

    lax.fori_loop(0, slices, one_slice, 0, unroll=2)


def both_halves(tile, low):
    return jnp.where(low, pltpu.roll(tile, 4, axis=0), tile)


def tiles_of(ref, *index):
    return [ref[(*index, slice(8 * t, 8 * t + 8))] for t in range(ROWS // 8)]


def composite(pieces, low):
    through = None
    for tiles in pieces:
        own = both_halves(tiles[-1], low)
        tiles = tiles[:-1] + [jnp.where(low, tiles[-1], 0.0)]
        if through is None:
            sums, through = tiles, own
        else:
            sums = [total + through * tile for total, tile in zip(sums, tiles)]
            through = through * own
    return sums[:-1] + [jnp.where(low, sums[-1], through)]


def merge(mine, other, mine_front, low):
    front = [jnp.where(mine_front, a, b) for a, b in zip(mine, other)]
    back = [jnp.where(mine_front, b, a) for a, b in zip(mine, other)]
    return composite([front, back], low)


def core_kernel(flips_ref, keep_ref, both_ref, mine_ref, send_ref):
    low = lax.broadcasted_iota(jnp.int32, (8, LANES), 0) < 4
    view = lax.axis_index("view")
    core, chip = view & 1, (view >> 1) & 1
    for k in range(keep_ref.shape[1]):
        mine_front = flips_ref[k] == core
        for half, out_ref in ((chip, mine_ref), (1 - chip, send_ref)):
            merged = merge(tiles_of(keep_ref, half, k), tiles_of(both_ref, 1 - core, half, k), mine_front, low)
            for t, tile in enumerate(merged):
                out_ref[k, 8 * t : 8 * t + 8, :] = tile


def chip_kernel(flips_ref, mine_ref, both_ref, out_ref):
    low = lax.broadcasted_iota(jnp.int32, (8, LANES), 0) < 4
    chip = (lax.axis_index("view") >> 1) & 1
    for k in range(mine_ref.shape[0]):
        merged = merge(tiles_of(mine_ref, k), tiles_of(both_ref, 1 - chip, k), flips_ref[k] == chip, low)
        for t, tile in enumerate(merged):
            out_ref[VIEW_ORDER.index(k), 8 * t : 8 * t + 8, :] = tile


def final_kernel(per_slice, flips_ref, shift_ref, color_ref, pieces_ref, out_ref, rows_ref):
    low = lax.broadcasted_iota(jnp.int32, (8, LANES), 0) < 4
    count = pieces_ref.shape[0]
    flipped = flips_ref[lax.axis_index("view") // per_slice] == 1
    ordered = []
    for j in range(count):
        near, far = tiles_of(pieces_ref, VIEW_ORDER.index(j)), tiles_of(pieces_ref, VIEW_ORDER.index(count - 1 - j))
        ordered.append([jnp.where(flipped, b, a) for a, b in zip(near, far)])
    first, second, third, blue, last = composite(ordered, low)
    blue_second = pltpu.roll(blue, 4, axis=0)
    opacity = 1.0 - last
    for light in range(LIGHTS):
        step = spread(shift_ref, 0, light)
        red_green = jnp.where(step == 0, second, jnp.where(step < 0, first, third))
        blues = jnp.where(step == 0, blue_second, jnp.where(step < 0, blue, last))
        tint = [spread(color_ref, c, light) for c in range(3)]
        rows_ref[light, 0:8, :] = red_green * jnp.where(low, tint[0], tint[1])
        rows_ref[light, 8:16, :] = jnp.where(low, blues * tint[2], opacity)
    for light in range(LIGHTS):
        for g in range(4):
            out_ref[light, :, g * LANES : (g + 1) * LANES] = rows_ref[light, pl.ds(g, 4, stride=4), :]


def vmem(count):
    return [pl.BlockSpec(memory_space=pltpu.VMEM)] * count


def local(density, albedo, light_color, light_shift, view_flip):
    slices, cells, columns = density.shape
    light_count, view_count = lax.axis_size("light"), lax.axis_size("view")
    light_scale = -LIGHT_DEPTH / (slices * light_count) * math.log2(math.e)
    view_scale = -VIEW_DEPTH / (cells * view_count) * math.log2(math.e)
    planes = len(STEPS) * cells
    f32 = jnp.float32

    def call(kernel, name, out_shape, in_specs, scratch=()):
        many = isinstance(out_shape, (list, tuple))
        return pl.pallas_call(
            kernel,
            name=name,
            out_shape=out_shape,
            in_specs=in_specs,
            out_specs=vmem(len(out_shape)) if many else vmem(1)[0],
            scratch_shapes=scratch,
            compiler_params=pltpu.CompilerParams(vmem_limit_bytes=16 * 2**20),
        )

    def shaped(*shape, kind=f32):
        return jax.ShapeDtypeStruct(shape, kind)

    lines = shaped(light_count, planes, columns // light_count)
    leaving = call(
        lambda *refs: exit_kernel(light_scale, *refs),
        "exits",
        lines,
        [pl.BlockSpec(memory_space=pltpu.HBM)],
        [
            pltpu.VMEM(density.shape, f32),
            pltpu.VMEM((len(STEPS), cells, columns), f32),
            pltpu.SemaphoreType.DMA((PARTS,)),
        ],
    )(pltpu.with_memory_space_constraint(density, pltpu.HBM))
    leaving, albedo = lax.optimization_barrier((leaving, albedo))
    along = [list(LIGHT_ORDER)]
    leaving = lax.all_to_all(leaving, "light", 0, 0, axis_index_groups=along)
    flip, shift, color = view_flip.reshape(1, -1), light_shift.reshape(1, -1), light_color.T
    entering, flips = call(
        lambda *refs: prefix_kernel(slices, *refs), "prefix", [lines, shaped(slices, 8, LANES, kind=jnp.int32)], vmem(4)
    )(leaving, flip, shift, color)
    entering = lax.all_to_all(entering, "light", 0, 0, axis_index_groups=along)
    keep, send = call(
        lambda *refs: brick_kernel(light_scale, view_scale, *refs),
        "brick",
        [shaped(2, slices, ROWS, LANES)] * 2,
        vmem(4),
        [
            pltpu.VMEM((len(STEPS), cells, columns), f32),
            pltpu.VMEM((len(STEPS), cells, columns), f32),
            pltpu.VMEM((columns // (4 * LANES) * ROWS * cells, LANES), f32),
        ],
    )(flips, density, albedo, entering)
    cores = [[2 * z, 2 * z + 1] for z in range(view_count // 2)]
    both = lax.all_gather(send, "view", axis_index_groups=cores)
    half = shaped(slices, ROWS, LANES)
    mine, send = call(core_kernel, "cores", [half] * 2, vmem(3))(flips, keep, both)
    chips = [[v, v + 2] for v in range(view_count) if v & 2 == 0]
    both = lax.all_gather(send, "view", axis_index_groups=chips)
    merged = call(chip_kernel, "chips", half, vmem(3))(flips, mine, both)
    rest = [[4 * k + r for k in VIEW_ORDER] for r in range(4)]
    pieces = lax.all_to_all(merged, "view", 0, 0, axis_index_groups=rest)
    return call(
        lambda *refs: final_kernel(view_count // slices, *refs),
        "final",
        shaped(LIGHTS, 4, slices * columns // view_count),
        vmem(4),
        [pltpu.VMEM((LIGHTS, 16, LANES), f32)],
    )(flips, shift, color, pieces)


def solution(mesh):
    return jax.shard_map(
        local,
        mesh=mesh,
        in_specs=(P("light", "view", None), P(None, "light", "view", None), P(), P(), P("light")),
        out_specs=P(None, None, ("light", "view")),
        check_vma=False,
    )
```

```python
import math

import jax
import jax.numpy as jnp
from jax import lax
from jax.experimental import pallas as pl
from jax.experimental.pallas import tpu as pltpu
from jax.sharding import PartitionSpec as P

LIGHTS = 8
LIGHT_DEPTH = 1.5
VIEW_DEPTH = 2.0
LANES = 128
STEPS = (-1, 0, 1)
CHANNELS = ((0, 0), (0, 1), (1, 0), (1, 1), (2, 0), (2, 1), (0, 2), (1, 2), (2, 2))
ROWS = 40
LIGHT_ORDER = (10, 9, 8, 7, 6, 5, 4, 3, 2, 1, 0, 15, 14, 13, 12, 11)
VIEW_ORDER = (5, 1, 3, 7, 0, 4, 2, 6)
PARTS = 2


def slide(planes, amount):
    if amount == 0:
        return planes
    columns = planes.shape[-1]
    rolled = pltpu.roll(planes, amount % columns, axis=1)
    lane = lax.broadcasted_iota(jnp.int32, (planes.shape[0], LANES), 1)
    if amount > 0:
        edge = jnp.where(lane >= amount, rolled[:, :LANES], 0.0)
        return jnp.concatenate([edge, rolled[:, LANES:]], axis=1)
    edge = jnp.where(lane < LANES + amount, rolled[:, columns - LANES :], 0.0)
    return jnp.concatenate([rolled[:, : columns - LANES], edge], axis=1)


def turn(groups, amount, forward):
    lane = lax.broadcasted_iota(jnp.int32, groups[0].shape, 1)
    if forward:
        spun = [pltpu.roll(g, lax.rem(amount, LANES), axis=1) for g in groups]
        return [jnp.where(lane >= amount, g, spun[i - 1]) for i, g in enumerate(spun)]
    spun = [pltpu.roll(g, lax.rem(LANES - amount, LANES), axis=1) for g in groups]
    return [jnp.where(lane < LANES - amount, g, spun[(i + 1) % len(spun)]) for i, g in enumerate(spun)]


def exit_kernel(scale, density_ref, exit_ref, dense_ref, total_ref, arrived):
    slices, cells, columns = density_ref.shape
    count = exit_ref.shape[0]
    size = slices // PARTS
    copies = []
    for part in range(PARTS):
        span = pl.ds(part * size, size)
        copies.append(pltpu.make_async_copy(density_ref.at[span], dense_ref.at[span], arrived.at[part]))
        copies[-1].start()
    amount = slices * (count - 1 - lax.axis_index("light"))
    for part, copy in enumerate(copies):
        copy.wait()
        for index, step in enumerate(STEPS):
            sums = [dense_ref[k] * scale for k in range(part * size, part * size + size)]
            reach = 1
            while len(sums) > 1:
                sums = [slide(a, reach * step) + b for a, b in zip(sums[::2], sums[1::2])]
                reach *= 2
            total_ref[index] = slide(total_ref[index], size * step) + sums[0] if part else sums[0]
    for index, step in enumerate(STEPS):
        total = slide(total_ref[index], step)
        groups = [total[:, g * LANES : (g + 1) * LANES] for g in range(count)]
        if step:
            groups = turn(groups, amount, step > 0)
        for g, values in enumerate(groups):
            exit_ref[g, index * cells : (index + 1) * cells, :] = values


def spread(ref, row, column):
    return jnp.broadcast_to(ref[row : row + 1, column : column + 1], (8, LANES))


def prefix_kernel(slices, leaving_ref, flip_ref, shift_ref, color_ref, entering_ref, flips_ref):
    for k in range(slices):
        flips_ref[k] = spread(flip_ref, 0, k)
    count, planes, _ = leaving_ref.shape
    cells = planes // len(STEPS)
    columns = count * LANES
    light = lax.axis_index("light")
    position = sum(jnp.where(light == member, p, 0) for p, member in enumerate(LIGHT_ORDER))
    place = position * LANES + lax.broadcasted_iota(jnp.int32, (cells, LANES), 1)
    for index, step in enumerate(STEPS):
        part = slice(index * cells, (index + 1) * cells)
        total = jnp.zeros((cells, LANES), jnp.float32)
        for j in range(count):
            member = LIGHT_ORDER.index(j)
            entering_ref[member, part, :] = total
            if step and j:
                column = (place - step * slices * (count - 1 - j) + columns) & (columns - 1)
                fresh = column < slices if step > 0 else column >= columns - slices
                total = jnp.where(fresh, 0.0, total)
            total = total + leaving_ref[member, part, :]


def gather_sums(parts, ref, base):
    for r, part in enumerate(parts):
        ref[base + 8 * r : base + 8 * r + 8, :] = part
    rows = [ref[pl.ds(base + y, 8, stride=8), :] for y in range(8)]
    while len(rows) > 1:
        rows = [a + b for a, b in zip(rows[::2], rows[1::2])]
    return rows[0]


def merged_rows(a, b, row, bit):
    mask = (row & (1 << bit)) == 0
    return jnp.where(mask, a, b) + pltpu.roll(jnp.where(mask, b, a), 1 << bit, axis=0)


def last_tile(parts, totals, row):
    sums = merged_rows(merged_rows(*parts[:2], row, 0), merged_rows(*parts[2:], row, 0), row, 1)
    depth = jnp.where(row == 4, totals[0], jnp.where(row == 5, totals[1], jnp.where(row == 6, totals[2], totals[3])))
    return jnp.where(row < 4, sums + pltpu.roll(sums, 4, axis=0), jnp.exp2(depth))


def brick_kernel(
    light_scale, view_scale, flips_ref, density_ref, albedo_ref, entering_ref, keep_ref, send_ref, depth_ref, lit_ref, turn_ref
):
    slices, cells, columns = density_ref.shape
    count = entering_ref.shape[0]
    core = lax.rem(lax.axis_index("view"), 2)
    light = lax.axis_index("light")
    for index, step in enumerate(STEPS):
        groups = [entering_ref[g, index * cells : (index + 1) * cells, :] for g in range(count)]
        if step:
            groups = turn(groups, slices * (count - light), step < 0)
        for g, values in enumerate(groups):
            depth_ref[index, :, g * LANES : (g + 1) * LANES] = values

    row = lax.broadcasted_iota(jnp.int32, (cells, LANES), 0)
    row_wide = lax.broadcasted_iota(jnp.int32, (cells, columns), 0)
    mine_even = core == 0

    def one_slice(k, carry):
        dense = density_ref[k]
        flipped = jnp.concatenate([flips_ref[k]] * (columns // LANES), axis=1) == 1
        depth_view = dense * view_scale
        running = depth_view
        for reach in (1, 2, 4):
            running = running + jnp.where(row_wide >= reach, pltpu.roll(running, reach, axis=0), 0.0)
        total = jnp.broadcast_to(running[cells - 1 :, :], (cells, columns))
        ahead = jnp.where(flipped, total - running, running - depth_view)
        weights = jnp.exp2(ahead) * (1.0 - jnp.exp2(depth_view))
        dense_light = dense * light_scale
        for index, step in enumerate(STEPS):
            depth = depth_ref[index]
            lit_ref[index] = weights * jnp.exp2(depth)
            depth_ref[index] = slide(depth + dense_light, step)
        for pair in range(columns // (8 * LANES)):
            chunks = []
            for chunk in (2 * pair, 2 * pair + 1):
                groups = [slice((4 * chunk + g) * LANES, (4 * chunk + g + 1) * LANES) for g in range(4)]
                reflect = [[albedo_ref[c, k, :, g].astype(jnp.float32) for g in groups] for c in range(3)]
                lit = [[lit_ref[index, :, g] for g in groups] for index in range(len(STEPS))]
                products = []
                for index, c in CHANNELS:
                    products += [reflect[c][g] * lit[index][g] for g in range(4)]
                tiles = [gather_sums(products[t : t + 8], turn_ref, 8 * (chunk * ROWS + t)) for t in range(0, ROWS - 8, 8)]
                tiles.append(last_tile(products[ROWS - 8 :], [total[:, g] for g in groups], row))
                chunks.append(tiles)
            for t, (even, odd) in enumerate(zip(*chunks)):
                keep_ref[pair, k, 8 * t : 8 * t + 8, :] = jnp.where(mine_even, even, odd)
                send_ref[pair, k, 8 * t : 8 * t + 8, :] = jnp.where(mine_even, odd, even)
        return carry

    lax.fori_loop(0, slices, one_slice, 0, unroll=2)


def both_halves(tile, low):
    return jnp.where(low, pltpu.roll(tile, 4, axis=0), tile)


def tiles_of(ref, *index):
    return [ref[(*index, slice(8 * t, 8 * t + 8))] for t in range(ROWS // 8)]


def composite(pieces, low):
    through = None
    for tiles in pieces:
        own = both_halves(tiles[-1], low)
        tiles = tiles[:-1] + [jnp.where(low, tiles[-1], 0.0)]
        if through is None:
            sums, through = tiles, own
        else:
            sums = [total + through * tile for total, tile in zip(sums, tiles)]
            through = through * own
    return sums[:-1] + [jnp.where(low, sums[-1], through)]


def merge(mine, other, mine_front, low):
    front = [jnp.where(mine_front, a, b) for a, b in zip(mine, other)]
    back = [jnp.where(mine_front, b, a) for a, b in zip(mine, other)]
    return composite([front, back], low)


def core_kernel(flips_ref, keep_ref, both_ref, mine_ref, send_ref):
    low = lax.broadcasted_iota(jnp.int32, (8, LANES), 0) < 4
    view = lax.axis_index("view")
    core, chip = view & 1, (view >> 1) & 1
    for k in range(keep_ref.shape[1]):
        mine_front = flips_ref[k] == core
        for half, out_ref in ((chip, mine_ref), (1 - chip, send_ref)):
            merged = merge(tiles_of(keep_ref, half, k), tiles_of(both_ref, 1 - core, half, k), mine_front, low)
            for t, tile in enumerate(merged):
                out_ref[k, 8 * t : 8 * t + 8, :] = tile


def chip_kernel(flips_ref, mine_ref, both_ref, out_ref):
    low = lax.broadcasted_iota(jnp.int32, (8, LANES), 0) < 4
    chip = (lax.axis_index("view") >> 1) & 1
    for k in range(mine_ref.shape[0]):
        merged = merge(tiles_of(mine_ref, k), tiles_of(both_ref, 1 - chip, k), flips_ref[k] == chip, low)
        for t, tile in enumerate(merged):
            out_ref[VIEW_ORDER.index(k), 8 * t : 8 * t + 8, :] = tile


def final_kernel(per_slice, flips_ref, shift_ref, color_ref, pieces_ref, out_ref, rows_ref):
    low = lax.broadcasted_iota(jnp.int32, (8, LANES), 0) < 4
    count = pieces_ref.shape[0]
    flipped = flips_ref[lax.axis_index("view") // per_slice] == 1
    ordered = []
    for j in range(count):
        near, far = tiles_of(pieces_ref, VIEW_ORDER.index(j)), tiles_of(pieces_ref, VIEW_ORDER.index(count - 1 - j))
        ordered.append([jnp.where(flipped, b, a) for a, b in zip(near, far)])
    first, second, third, blue, last = composite(ordered, low)
    blue_second = pltpu.roll(blue, 4, axis=0)
    opacity = 1.0 - last
    for light in range(LIGHTS):
        step = spread(shift_ref, 0, light)
        red_green = jnp.where(step == 0, second, jnp.where(step < 0, first, third))
        blues = jnp.where(step == 0, blue_second, jnp.where(step < 0, blue, last))
        tint = [spread(color_ref, c, light) for c in range(3)]
        rows_ref[light, 0:8, :] = red_green * jnp.where(low, tint[0], tint[1])
        rows_ref[light, 8:16, :] = jnp.where(low, blues * tint[2], opacity)
    for light in range(LIGHTS):
        for g in range(4):
            out_ref[light, :, g * LANES : (g + 1) * LANES] = rows_ref[light, pl.ds(g, 4, stride=4), :]


def vmem(count):
    return [pl.BlockSpec(memory_space=pltpu.VMEM)] * count


def local(density, albedo, light_color, light_shift, view_flip):
    slices, cells, columns = density.shape
    light_count, view_count = lax.axis_size("light"), lax.axis_size("view")
    light_scale = -LIGHT_DEPTH / (slices * light_count) * math.log2(math.e)
    view_scale = -VIEW_DEPTH / (cells * view_count) * math.log2(math.e)
    planes = len(STEPS) * cells
    f32 = jnp.float32

    def call(kernel, name, out_shape, in_specs, scratch=()):
        many = isinstance(out_shape, (list, tuple))
        return pl.pallas_call(
            kernel,
            name=name,
            out_shape=out_shape,
            in_specs=in_specs,
            out_specs=vmem(len(out_shape)) if many else vmem(1)[0],
            scratch_shapes=scratch,
            compiler_params=pltpu.CompilerParams(vmem_limit_bytes=16 * 2**20),
        )

    def shaped(*shape, kind=f32):
        return jax.ShapeDtypeStruct(shape, kind)

    lines = shaped(light_count, planes, columns // light_count)
    leaving = call(
        lambda *refs: exit_kernel(light_scale, *refs),
        "exits",
        lines,
        [pl.BlockSpec(memory_space=pltpu.HBM)],
        [
            pltpu.VMEM(density.shape, f32),
            pltpu.VMEM((len(STEPS), cells, columns), f32),
            pltpu.SemaphoreType.DMA((PARTS,)),
        ],
    )(pltpu.with_memory_space_constraint(density, pltpu.HBM))
    leaving, albedo = lax.optimization_barrier((leaving, albedo))
    along = [list(LIGHT_ORDER)]
    leaving = lax.all_to_all(leaving, "light", 0, 0, axis_index_groups=along)
    flip, shift, color = view_flip.reshape(1, -1), light_shift.reshape(1, -1), light_color.T
    entering, flips = call(
        lambda *refs: prefix_kernel(slices, *refs), "prefix", [lines, shaped(slices, 8, LANES, kind=jnp.int32)], vmem(4)
    )(leaving, flip, shift, color)
    entering = lax.all_to_all(entering, "light", 0, 0, axis_index_groups=along)
    keep, send = call(
        lambda *refs: brick_kernel(light_scale, view_scale, *refs),
        "brick",
        [shaped(2, slices, ROWS, LANES)] * 2,
        vmem(4),
        [
            pltpu.VMEM((len(STEPS), cells, columns), f32),
            pltpu.VMEM((len(STEPS), cells, columns), f32),
            pltpu.VMEM((columns // (4 * LANES) * ROWS * cells, LANES), f32),
        ],
    )(flips, density, albedo, entering)
    cores = [[2 * z, 2 * z + 1] for z in range(view_count // 2)]
    both = lax.all_gather(send, "view", axis_index_groups=cores)
    half = shaped(slices, ROWS, LANES)
    mine, send = call(core_kernel, "cores", [half] * 2, vmem(3))(flips, keep, both)
    chips = [[v, v + 2] for v in range(view_count) if v & 2 == 0]
    both = lax.all_gather(send, "view", axis_index_groups=chips)
    merged = call(chip_kernel, "chips", half, vmem(3))(flips, mine, both)
    rest = [[4 * k + r for k in VIEW_ORDER] for r in range(4)]
    pieces = lax.all_to_all(merged, "view", 0, 0, axis_index_groups=rest)
    return call(
        lambda *refs: final_kernel(view_count // slices, *refs),
        "final",
        shaped(LIGHTS, 4, slices * columns // view_count),
        vmem(4),
        [pltpu.VMEM((LIGHTS, 16, LANES), f32)],
    )(flips, shift, color, pieces)


def solution(mesh):
    return jax.shard_map(
        local,
        mesh=mesh,
        in_specs=(P("light", "view", None), P(None, "light", "view", None), P(), P(), P("light")),
        out_specs=P(None, None, ("light", "view")),
        check_vma=False,
    )
```
